32 devices in a mesh: grp: 4 (over y, x), dev: 8 (over z, core).
Axes of the slice: x: 2, y: 2, z: 4, core: 2. Of those that a mesh axis runs over, the one named last changes fastest.
Arguments:
- tiles: bfloat16 [128, 9, 4, 4, 128], P(('grp', 'dev')), may hold values from -6 to 6
- cotangent: bfloat16 [128, 9, 8, 8, 128], P(('grp', 'dev')), may hold values from -6 to 6
- weight: bfloat16 [3456, 128], P('dev'), may hold values from -0.109375 to 0.109375
- bias: float32 [128], replicated, may hold values from -4 to 4
- counts: int32 [32], replicated, may hold values from 1 to 4, as said below
Outputs:
- grad_weight: float32 [3456, 128], P('dev')
- grad_bias: float32 [128], P('dev')
The draws below stay inside these ranges and needn't reach their ends.
Inputs may be any that keep to these rules, and one draw needn't show every extreme that they name: `counts`: every group of 8 devices has at least one device with 4 live tiles; live tiles fill the first slots of a device.
All inputs are finite; a program needn't handle non-finite values.
Results may differ from the reference program's by a relative error of at most 0.0049.
Values may be sent and summed in bfloat16 or wider, within the bound.
A program may use at most 64 MiB of HBM per device.

```python
import jax
import jax.numpy as jnp
from jax import lax

CIN = 128
COUT = 128
F = 9
HL = 4
WL = 4
CAP = 4
SLOTS = 128
N_GRP = 4
N_DEV = 8


def draw_counts(key, part):
    total = N_GRP * N_DEV
    first, second = jax.random.split(jax.random.fold_in(key, 17))
    heavy = jax.random.randint(first, (total,), 0, 5) == 0
    base = jnp.where(heavy, CAP, 1).astype(jnp.int32).reshape(N_GRP, N_DEV)
    chosen = jax.random.randint(second, (N_GRP,), 0, N_DEV)
    forced = jnp.arange(N_DEV)[None, :] == chosen[:, None]
    return jnp.where(forced, CAP, base).astype(jnp.int32).reshape(total)


def spiked(array, key, source, target, shards_of, factor):
    owner, partner = [(jnp.arange(array.shape[dim]) // (array.shape[dim] // shards_of)).reshape([-1 if axis == dim else 1 for axis in range(array.ndim)]) for dim in (source, target)]
    chosen = jax.random.permutation(key, shards_of)[partner]
    strong = (owner == chosen) | (owner == (partner + shards_of // 2) % shards_of)
    return jnp.where(strong, factor * array, array)


def block_levels(stream_key, shape, shards, least, largest):
    gain = 1.0
    for dim, shards_of in shards:
        draws = jax.random.uniform(jax.random.fold_in(jax.random.fold_in(stream_key, 6), dim), (shards_of,), jnp.float32, least / len(shards), largest / len(shards))
        gain = gain * jnp.repeat(jnp.exp(draws), shape[dim] // shards_of).reshape((-1,) + (1,) * (len(shape) - 1 - dim))
    return gain


def scatter_about(stream_key, dims, scale, limit, cuts=(), kind=jnp.bfloat16):
    entries = jax.random.normal(stream_key, dims, jnp.float32) * scale
    if len(cuts) > 0:
        entries = block_levels(stream_key, dims, cuts, -0.22, 0.18) * entries
    return jnp.clip(entries, min=-limit, max=limit).astype(kind)


def bell_draw_with(key, dims, scale, reach, shards, heavy, kind=jnp.bfloat16):
    values = scale * jax.random.normal(key, dims, jnp.float32)
    if shards:
        values = values * block_levels(key, dims, shards, -0.22, 0.18)
    return jnp.clip(spiked(values, jax.random.fold_in(key, 3), *heavy), -reach, reach).astype(kind)


def setup_inputs(seed: int = 0) -> dict:
    keys = jax.random.split(jax.random.key(seed), 6)
    return {
        "tiles": bell_draw_with(keys[0], (SLOTS, F, HL, WL, CIN), 1.0, 6.0, ((0, 32),), (0, 4, 32, 2.75)),
        "cotangent": scatter_about(keys[1], (SLOTS, F, 2 * HL, 2 * WL, COUT), 1.0, 6.0, ((0, 32),)),
        "weight": scatter_about(keys[2], (27 * CIN, COUT), (27 * CIN) ** -0.5, 0.109375, ((0, 8),)),
        "bias": scatter_about(keys[3], (COUT,), 1.0, 4.0, (), jnp.float32),
        "counts": draw_counts(jax.random.fold_in(keys[5], 71), 0),
    }


def padded_input(tile):
    up = jnp.repeat(jnp.repeat(tile, 2, axis=1), 2, axis=2)
    up = jnp.concatenate([up[:1], up[:1], up], axis=0)
    return jnp.pad(up, ((0, 0), (1, 1), (1, 1), (0, 0)))

def window_list(padded, frames, height, width):
    chans = padded.shape[-1]
    result = []
    for kd in range(3):
        for kh in range(3):
            for kw in range(3):
                piece = padded[kd:kd + frames, kh:kh + height, kw:kw + width, :]
                result.append(piece.reshape(frames * height * width, chans))
    return result

def tile_terms(tile, cot, taps, bias):
    frames, height, width = (tile.shape[0], 2 * tile.shape[1], 2 * tile.shape[2])
    windows = window_list(padded_input(tile), frames, height, width)
    z = jnp.zeros((frames * height * width, taps.shape[2]), jnp.float32) + bias.astype(jnp.float32)
    for k in range(27):
        z = z + jnp.dot(windows[k], taps[k], preferred_element_type=jnp.float32)
    sig = jax.nn.sigmoid(z)
    dz = (cot.reshape(z.shape).astype(jnp.float32) * sig * (1.0 + z * (1.0 - sig))).astype(jnp.bfloat16)
    grads = [lax.dot_general(windows[k], dz, (((0,), (0,)), ((), ())), preferred_element_type=jnp.float32) for k in range(27)]
    return (jnp.stack(grads, 0), lax.optimization_barrier(jnp.sum(dz.astype(jnp.float32), axis=0)))

def reference(tiles, cotangent, weight, bias, counts):
    cin = tiles.shape[-1]
    cout = weight.shape[1]
    taps = weight.reshape(cin, 27, cout).transpose(1, 0, 2)
    slots = tiles.shape[0]
    cap = slots // counts.shape[0]
    cells = tiles.shape[1] * 4 * tiles.shape[2] * tiles.shape[3]
    scale = 1.0 / jnp.sqrt(jnp.float32(slots * cells))

    def step(carry, index):
        live = index % cap < counts[index // cap]

        def compute(args):
            return tile_terms(tiles[index], cotangent[index], taps, bias)

        def skip(args):
            return (jnp.zeros((27, cin, cout), jnp.float32), jnp.zeros((cout,), jnp.float32))
        gw, gb = lax.cond(live, compute, skip, 0)
        return ((carry[0] + gw, carry[1] + gb), None)
    init = (jnp.zeros((27, cin, cout), jnp.float32), jnp.zeros((cout,), jnp.float32))
    (gw, gb), _ = lax.scan(step, init, jnp.arange(slots, dtype=jnp.int32))
    grad_weight = gw.transpose(1, 0, 2).reshape(cin * 27, cout) * scale
    return (grad_weight, gb * scale)
```

```python
import functools
import math

import jax
import jax.numpy as jnp
from jax import lax
from jax.experimental import pallas as pl
from jax.experimental.pallas import tpu as pltpu
from jax.sharding import PartitionSpec as P

MESH = pl.DeviceIdType.MESH
TAPS = {(0, 0): (0,), (0, 1): (1, 2), (1, 0): (0, 1), (1, 1): (2,)}
OFFSET = ((0, 1, 1), (0, 0, 1))


def terms_kernel(w_ref, x_ref, cot_ref, bias_ref, out_ref, wz_ref, g_ref):
    chans = 128
    slab = x_ref.shape[0] // 6
    rows = 4 * slab
    cols = ((0, 256), (0, 512), (256, 256))

    wz_ref[...] = jnp.zeros_like(wz_ref)
    for kd in range(3):
        tap = {}
        for kh in range(3):
            for kw in range(3):
                piece = w_ref[:, 9 * kd + 3 * kh + kw]
                tap[kh, kw] = piece.reshape(chans, chans).astype(jnp.float32)
        for ph in range(2):
            for a in range(2):
                line = [sum(tap[kh, kw] for kh in TAPS[ph, a]) for kw in range(3)]
                for pw in range(2):
                    for b in range(2):
                        both = sum(line[kw] for kw in TAPS[pw, b])
                        row = (b + pw) * 384 + kd * 128
                        col = (2 * ph + pw) * 128
                        wz_ref[a + ph, row : row + 128, col : col + 128] = both.astype(
                            jnp.bfloat16
                        )

    def window(dh):
        return x_ref[dh * slab : dh * slab + rows, :]

    mid = jnp.dot(window(1), wz_ref[1], preferred_element_type=jnp.float32)
    top = jnp.dot(window(0), wz_ref[0, :, 0:256], preferred_element_type=jnp.float32)
    low = jnp.dot(window(2), wz_ref[2, :, 256:512], preferred_element_type=jnp.float32)
    parts = []
    total_b = jnp.zeros((1, chans), jnp.float32)
    for p in range(4):
        side = (top if p < 2 else low)[:, (p % 2) * 128 : (p % 2) * 128 + 128]
        z = mid[:, p * 128 : p * 128 + 128] + side + bias_ref[...]
        sig = jax.nn.sigmoid(z)
        dz = cot_ref[p].astype(jnp.float32) * sig * (1.0 + z * (1.0 - sig))
        dz = dz.astype(jnp.bfloat16)
        total_b += jnp.sum(dz.astype(jnp.float32), axis=0, keepdims=True)
        parts.append(dz)
    dz = jnp.concatenate(parts, axis=1)
    for dh in range(3):
        start, width = cols[dh]
        g_ref[dh, :, start : start + width] = lax.dot_general(
            window(dh),
            dz[:, start : start + width],
            (((0,), (0,)), ((), ())),
            preferred_element_type=jnp.float32,
        )
    for kd in range(3):
        for kh in range(3):
            for kw in range(3):
                total = None
                for ph in range(2):
                    for pw in range(2):
                        row = (OFFSET[pw][kw] + pw) * 384 + kd * 128
                        col = (2 * ph + pw) * 128
                        term = g_ref[
                            OFFSET[ph][kh] + ph, row : row + 128, col : col + 128
                        ]
                        total = term if total is None else total + term
                out_ref[:, 9 * kd + 3 * kh + kw] = total.reshape(8, 16, chans)
    out_ref[:, 27] = jnp.broadcast_to(total_b.reshape(1, 1, chans), (8, 16, chans))


def terms(w, xs, cot, bias):
    flops = 2 * 2 * 576 * 1152 * 1024
    return pl.pallas_call(
        terms_kernel,
        out_shape=jax.ShapeDtypeStruct((8, 28, 16, 128), jnp.float32),
        in_specs=[pl.BlockSpec(memory_space=pltpu.VMEM)] * 4,
        out_specs=pl.BlockSpec(memory_space=pltpu.VMEM),
        scratch_shapes=[
            pltpu.VMEM((3, 1152, 512), jnp.bfloat16),
            pltpu.VMEM((3, 1152, 512), jnp.float32),
        ],
        compiler_params=pltpu.CompilerParams(vmem_limit_bytes=48 * 2**20),
        cost_estimate=pl.CostEstimate(
            flops=flops, bytes_accessed=6 * 2**20, transcendentals=576 * 512
        ),
    )(w, xs, cot, bias)


def reduce_kernel(
    scale, x_ref, o_ref, s1, r1, s2, r2, keep, s3, r3, s4, r4,
    ss1, rs1, ss2, rs2, ss3, rs3, ss4, rs4,
):
    grp = lax.axis_index("grp")
    dev = lax.axis_index("dev")
    depth = dev // 2
    core = dev % 2
    f32, bf16 = jnp.float32, jnp.bfloat16
    pair = {"dev": depth * 2 + (1 - core)}
    across = [{"grp": (grp + k) % 4} for k in range(1, 4)]
    along = [{"dev": ((depth + k) % 4) * 2 + core} for k in range(1, 4)]

    barrier = pltpu.get_barrier_semaphore()
    for peer in [pair] + across + along:
        pl.semaphore_signal(barrier, inc=1, device_id=peer, device_id_type=MESH)

    def send(src, dst, ssem, rsem, peer):
        copy = pltpu.make_async_remote_copy(
            src_ref=src, dst_ref=dst, send_sem=ssem, recv_sem=rsem,
            device_id=peer, device_id_type=MESH,
        )
        copy.start()
        return copy

    copies = []
    first = []
    for k in range(4):
        taps = pl.ds(((grp + k + 1) % 4) * 7, 7)
        s1[k] = x_ref[:, 1 - core, taps].astype(bf16)
        if k == 0:
            pl.semaphore_wait(barrier, 7)
        first.append(send(s1.at[k], r1.at[k], ss1.at[k], rs1.at[k], pair))
    second = []
    for k in range(4):
        taps = pl.ds(((grp + k + 1) % 4) * 7, 7)
        first[k].wait_recv()
        total = x_ref[:, core, taps] + r1[k].astype(f32)
        if k < 3:
            s2[k] = total.astype(bf16)
            second.append(send(s2.at[k], r2.at[k], ss2.at[k], rs2.at[k], across[k]))
        else:
            keep[...] = total
    for k in range(3):
        second[k].wait_recv()
        keep[...] += r2[k].astype(f32)
    third = []
    for k in range(3):
        s3[k] = keep[(depth + k + 1) % 4].astype(bf16)
        third.append(send(s3.at[k], r3.at[k], ss3.at[k], rs3.at[k], along[k]))
    total = keep[depth]
    for k in range(3):
        third[k].wait_recv()
        total += r3[k].astype(f32)
    total = total * scale
    s4[...] = total
    fourth = [
        send(s4, r4.at[k], ss4.at[k], rs4.at[k], across[k]) for k in range(3)
    ]
    o_ref[grp] = total
    for k in range(3):
        fourth[k].wait_recv()
        o_ref[(grp + 3 - k) % 4] = r4[k]
    for copy in first + second + third + fourth:
        copy.wait_send()


def reduce_terms(parts, scale):
    bf16, f32 = jnp.bfloat16, jnp.float32
    sem = pltpu.SemaphoreType.DMA
    return pl.pallas_call(
        functools.partial(reduce_kernel, scale),
        out_shape=jax.ShapeDtypeStruct((4, 7, 16, 128), f32),
        in_specs=[pl.BlockSpec(memory_space=pltpu.VMEM)],
        out_specs=pl.BlockSpec(memory_space=pltpu.VMEM),
        scratch_shapes=[
            pltpu.VMEM((4, 4, 7, 16, 128), bf16),
            pltpu.VMEM((4, 4, 7, 16, 128), bf16),
            pltpu.VMEM((3, 4, 7, 16, 128), bf16),
            pltpu.VMEM((3, 4, 7, 16, 128), bf16),
            pltpu.VMEM((4, 7, 16, 128), f32),
            pltpu.VMEM((3, 7, 16, 128), bf16),
            pltpu.VMEM((3, 7, 16, 128), bf16),
            pltpu.VMEM((7, 16, 128), f32),
            pltpu.VMEM((3, 7, 16, 128), f32),
            sem((4,)), sem((4,)), sem((3,)), sem((3,)),
            sem((3,)), sem((3,)), sem((3,)), sem((3,)),
        ],
        compiler_params=pltpu.CompilerParams(
            collective_id=1, has_side_effects=True, vmem_limit_bytes=48 * 2**20
        ),
    )(parts.reshape(4, 2, 28, 16, 128))


def input_windows(tiles):
    xt = tiles.transpose(2, 3, 0, 1, 4)
    first = xt[:, :, :, :1]
    back1 = jnp.concatenate([first, xt[:, :, :, :-1]], axis=3)
    back2 = jnp.concatenate([first, first, xt[:, :, :, :-2]], axis=3)
    timed = jnp.concatenate([back2, back1, xt], axis=-1)
    padded = jnp.pad(timed, ((1, 1), (1, 1), (0, 0), (0, 0), (0, 0)))
    wide = jnp.concatenate([padded[:, dw : dw + 4] for dw in range(3)], axis=-1)
    return wide.reshape(-1, wide.shape[-1])


def body(tiles, cotangent, weight, bias, counts):
    num_dev = lax.axis_size("dev")
    num_grp = lax.axis_size("grp")
    cap, frames, hl, wl, cin = tiles.shape
    cout = weight.shape[1]
    my_dev = lax.axis_index("dev")
    my_grp = lax.axis_index("grp")
    scale = 1.0 / math.sqrt(cap * num_dev * num_grp * frames * 4 * hl * wl)

    mine = weight.reshape(cin // num_dev, 27, cout).transpose(1, 0, 2)
    gathered = lax.all_gather(mine, "dev", axis=0, tiled=False)
    if num_dev != 8:
        gathered = gathered.transpose(1, 0, 2, 3).reshape(27, 8, 16, cout)
        gathered = gathered.transpose(1, 0, 2, 3)

    xs = input_windows(tiles)
    my_count = counts[my_grp * num_dev + my_dev]
    live = (jnp.arange(cap, dtype=jnp.int32) < my_count).reshape(cap, 1, 1, 1, 1)
    cot = jnp.where(live, cotangent, jnp.zeros((), cotangent.dtype))
    cot = cot.reshape(cap, frames, hl, 2, wl, 2, cout).transpose(3, 5, 2, 4, 0, 1, 6)
    cot = cot.reshape(4, hl * wl * cap * frames, cout)

    parts = terms(gathered, xs, cot, bias.reshape(1, cout))
    share = cout // num_dev
    if (num_grp, num_dev) == (4, 8):
        done = reduce_terms(parts, scale).reshape(28, 16, cout)
        part_w = done[:27].transpose(1, 0, 2).reshape(432, cout)
        part_b = lax.dynamic_slice_in_dim(done[27, 0], my_dev * share, share, 0)
        return part_w, part_b
    flat = parts[:, :27].transpose(0, 2, 1, 3).reshape(cin * 27, cout)
    part_w = lax.psum_scatter(flat, "dev", scatter_dimension=0, tiled=True)
    part_w = lax.psum(part_w, "grp")
    total_b = lax.psum(parts[0, 27, 0], ("grp", "dev"))
    part_b = lax.dynamic_slice_in_dim(total_b, my_dev * share, share, 0)
    return part_w * scale, part_b * scale


def solution(mesh):
    return jax.shard_map(
        body,
        mesh=mesh,
        in_specs=(
            P(("grp", "dev"), None, None, None, None),
            P(("grp", "dev"), None, None, None, None),
            P("dev", None),
            P(),
            P(),
        ),
        out_specs=(P("dev", None), P("dev")),
        check_vma=False,
    )
```

```python
import functools
import math

import jax
import jax.numpy as jnp
from jax import lax
from jax.experimental import pallas as pl
from jax.experimental.pallas import tpu as pltpu
from jax.sharding import PartitionSpec as P

MESH = pl.DeviceIdType.MESH
TAPS = {(0, 0): (0,), (0, 1): (1, 2), (1, 0): (0, 1), (1, 1): (2,)}
OFFSET = ((0, 1, 1), (0, 0, 1))


def build_windows(x_ref, f_ref, xs_ref):
    rows = x_ref.shape[0]
    slab = rows // 4
    pad = 40
    row = lax.broadcasted_iota(jnp.int32, (rows, 128), 0).astype(jnp.float32)
    frame = row - 9.0 * jnp.floor((row + 0.5) * (1.0 / 9.0))
    place = lax.broadcasted_iota(jnp.int32, (slab, 128), 0)
    xs_ref[0:slab] = jnp.zeros((slab, 1152), jnp.bfloat16)
    xs_ref[5 * slab : 6 * slab] = jnp.zeros((slab, 1152), jnp.bfloat16)
    f_ref[...] = jnp.zeros_like(f_ref)
    now = x_ref[...].astype(jnp.float32)
    f_ref[2, pad : pad + rows] = now
    back1 = jnp.where(frame < 0.5, now, f_ref[2, pad - 1 : pad - 1 + rows])
    f_ref[1, pad : pad + rows] = back1
    f_ref[0, pad : pad + rows] = jnp.where(
        frame < 1.5, back1, f_ref[2, pad - 2 : pad - 2 + rows]
    )
    for h in range(4):
        for dw in range(3):
            for kd in range(3):
                start = pad + h * slab + (dw - 1) * 36
                piece = f_ref[kd, start : start + slab]
                if dw == 0:
                    piece = jnp.where(place < 36, 0.0, piece)
                if dw == 2:
                    piece = jnp.where(place >= slab - 36, 0.0, piece)
                col = dw * 384 + kd * 128
                xs_ref[(h + 1) * slab : (h + 2) * slab, col : col + 128] = piece.astype(
                    jnp.bfloat16
                )


def combine_weights(w_ref, wz_ref):
    chans = 128
    for kd in range(3):
        tap = {}
        for kh in range(3):
            for kw in range(3):
                piece = w_ref[:, 9 * kd + 3 * kh + kw]
                tap[kh, kw] = piece.reshape(chans, chans).astype(jnp.float32)
        for ph in range(2):
            for a in range(2):
                line = [sum(tap[kh, kw] for kh in TAPS[ph, a]) for kw in range(3)]
                for pw in range(2):
                    for b in range(2):
                        both = sum(line[kw] for kw in TAPS[pw, b])
                        row = (b + pw) * 384 + kd * 128
                        col = (2 * ph + pw) * 128
                        wz_ref[a + ph, row : row + 128, col : col + 128] = both.astype(
                            jnp.bfloat16
                        )


def products(xs_ref, cot_ref, bias_ref, wz_ref, g_ref):
    slab = xs_ref.shape[0] // 6
    rows = 4 * slab
    cols = ((0, 256), (0, 512), (256, 256))

    def window(dh):
        return xs_ref[dh * slab : dh * slab + rows, :]

    mid = jnp.dot(window(1), wz_ref[1], preferred_element_type=jnp.float32)
    top = jnp.dot(window(0), wz_ref[0, :, 0:256], preferred_element_type=jnp.float32)
    low = jnp.dot(window(2), wz_ref[2, :, 256:512], preferred_element_type=jnp.float32)
    parts = []
    total_b = jnp.zeros((1, 128), jnp.float32)
    for p in range(4):
        side = (top if p < 2 else low)[:, (p % 2) * 128 : (p % 2) * 128 + 128]
        z = mid[:, p * 128 : p * 128 + 128] + side + bias_ref[...]
        sig = jax.nn.sigmoid(z)
        dz = cot_ref[p].astype(jnp.float32) * sig * (1.0 + z * (1.0 - sig))
        dz = dz.astype(jnp.bfloat16)
        total_b += jnp.sum(dz.astype(jnp.float32), axis=0, keepdims=True)
        parts.append(dz)
    dz = jnp.concatenate(parts, axis=1)
    for dh in range(3):
        start, width = cols[dh]
        g_ref[dh, :, start : start + width] = lax.dot_general(
            window(dh),
            dz[:, start : start + width],
            (((0,), (0,)), ((), ())),
            preferred_element_type=jnp.float32,
        )
    return total_b


def tap_gradient(g_ref, k):
    kd, kh, kw = k // 9, k // 3 % 3, k % 3
    total = None
    for ph in range(2):
        for pw in range(2):
            row = (OFFSET[pw][kw] + pw) * 384 + kd * 128
            col = (2 * ph + pw) * 128
            term = g_ref[OFFSET[ph][kh] + ph, row : row + 128, col : col + 128]
            total = term if total is None else total + term
    return total


WORK = [
    pltpu.VMEM((3, 656, 128), jnp.float32),
    pltpu.VMEM((864, 1152), jnp.bfloat16),
    pltpu.VMEM((3, 1152, 512), jnp.bfloat16),
    pltpu.VMEM((3, 1152, 512), jnp.float32),
]


def terms_kernel(w_ref, x_ref, cot_ref, bias_ref, out_ref, f_ref, xs_ref, wz_ref, g_ref):
    build_windows(x_ref, f_ref, xs_ref)
    wz_ref[...] = jnp.zeros_like(wz_ref)
    combine_weights(w_ref, wz_ref)
    total_b = products(xs_ref, cot_ref, bias_ref, wz_ref, g_ref)
    for k in range(27):
        out_ref[:, k] = tap_gradient(g_ref, k).reshape(8, 16, 128)
    out_ref[:, 27] = jnp.broadcast_to(total_b.reshape(1, 1, 128), (8, 16, 128))


def terms(w, x, cot, bias):
    return pl.pallas_call(
        terms_kernel,
        out_shape=jax.ShapeDtypeStruct((8, 28, 16, 128), jnp.float32),
        in_specs=[pl.BlockSpec(memory_space=pltpu.VMEM)] * 4,
        out_specs=pl.BlockSpec(memory_space=pltpu.VMEM),
        scratch_shapes=WORK,
        compiler_params=pltpu.CompilerParams(vmem_limit_bytes=48 * 2**20),
    )(w, x, cot, bias)


def whole_kernel(
    scale, w_ref, x_ref, cot_ref, bias_ref, o_ref, b_ref,
    f_ref, xs_ref, wz_ref, g_ref, w_all, parts,
    s1, r1, s2, r2, keep, s3, r3, s4, r4, sb, rb,
    sw1, rw1, sw2, rw2, ss1, rs1, ss2, rs2, ss3, rs3, ss4, rs4, ssb, rsb,
):
    grp = lax.axis_index("grp")
    dev = lax.axis_index("dev")
    depth = dev // 2
    core = dev % 2
    f32, bf16 = jnp.float32, jnp.bfloat16
    pair = {"dev": depth * 2 + (1 - core)}
    across = [{"grp": (grp + k) % 4} for k in range(1, 4)]
    along = [{"dev": ((depth + k) % 4) * 2 + core} for k in range(1, 4)]

    barrier = pltpu.get_barrier_semaphore()
    for peer in [pair] + across + along:
        pl.semaphore_signal(barrier, inc=1, device_id=peer, device_id_type=MESH)
    pl.semaphore_wait(barrier, 7)

    def send(src, dst, ssem, rsem, peer):
        copy = pltpu.make_async_remote_copy(
            src_ref=src, dst_ref=dst, send_sem=ssem, recv_sem=rsem,
            device_id=peer, device_id_type=MESH,
        )
        copy.start()
        return copy

    out = [
        send(w_ref, w_all.at[dev], sw1.at[k], rw1.at[k], along[k]) for k in range(3)
    ]
    swap = [send(w_ref, w_all.at[dev], sw2.at[3], rw2.at[3], pair)]
    w_all[dev] = w_ref[...]
    wz_ref[...] = jnp.zeros_like(wz_ref)
    build_windows(x_ref, f_ref, xs_ref)
    for k in (0, 2, 1):
        out[k].wait_recv()
        block = w_all.at[((depth + 3 - k) % 4) * 2 + core]
        swap.append(send(block, block, sw2.at[k], rw2.at[k], pair))
    for copy in swap:
        copy.wait_recv()
    combine_weights(w_all, wz_ref)
    total_b = products(xs_ref, cot_ref, bias_ref, wz_ref, g_ref)

    sb[0] = jnp.broadcast_to(total_b, (8, 128))
    bias_copies = [send(sb.at[0], rb.at[0], ssb.at[0], rsb.at[0], pair)]
    first = []
    for q in range(4):
        for k in range(7 * q, 7 * q + 7):
            if k < 27:
                parts[:, :, k] = tap_gradient(g_ref, k).reshape(4, 2, 16, 128)
            else:
                parts[:, :, k] = jnp.zeros((4, 2, 16, 128), f32)
        s1[q] = parts[:, 1 - core, 7 * q : 7 * q + 7].astype(bf16)
        first.append(send(s1.at[q], r1.at[q], ss1.at[q], rs1.at[q], pair))

    bias_copies[0].wait_recv()
    sb[1] = sb[0] + rb[0]
    for k in range(3):
        bias_copies.append(
            send(sb.at[1], rb.at[1 + k], ssb.at[1 + k], rsb.at[1 + k], across[k])
        )
    second = []
    for q in range(4):
        first[q].wait_recv()
    for k in range(4):
        q = (grp + k + 1) % 4
        total = parts[:, core, pl.ds(q * 7, 7)] + r1[q].astype(f32)
        if k < 3:
            s2[k] = total.astype(bf16)
            second.append(send(s2.at[k], r2.at[k], ss2.at[k], rs2.at[k], across[k]))
        else:
            keep[...] = total
    for k in range(3):
        bias_copies[1 + k].wait_recv()
    sb[2] = (sb[1] + rb[1]) + (rb[2] + rb[3])
    for k in range(3):
        bias_copies.append(
            send(sb.at[2], rb.at[4 + k], ssb.at[4 + k], rsb.at[4 + k], along[k])
        )
    for k in range(3):
        second[k].wait_recv()
        keep[...] += r2[k].astype(f32)
    third = []
    for k in range(3):
        s3[k] = keep[(depth + k + 1) % 4].astype(bf16)
        third.append(send(s3.at[k], r3.at[k], ss3.at[k], rs3.at[k], along[k]))
    for k in range(3):
        bias_copies[4 + k].wait_recv()
    b_ref[...] = ((sb[2] + rb[4]) + (rb[5] + rb[6])) * scale
    total = keep[depth]
    for k in range(3):
        third[k].wait_recv()
        total += r3[k].astype(f32)
    total = total * scale
    s4[...] = total
    fourth = [
        send(s4, r4.at[k], ss4.at[k], rs4.at[k], across[k]) for k in range(3)
    ]
    o_ref[grp] = total
    for k in range(3):
        fourth[k].wait_recv()
        o_ref[(grp + 3 - k) % 4] = r4[k]
    for copy in out + swap + bias_copies + first + second + third + fourth:
        copy.wait_send()


def whole(w, x, cot, bias, scale):
    bf16, f32 = jnp.bfloat16, jnp.float32
    sem = pltpu.SemaphoreType.DMA
    return pl.pallas_call(
        functools.partial(whole_kernel, scale),
        out_shape=(
            jax.ShapeDtypeStruct((4, 7, 16, 128), f32),
            jax.ShapeDtypeStruct((8, 128), f32),
        ),
        in_specs=[pl.BlockSpec(memory_space=pltpu.VMEM)] * 4,
        out_specs=[pl.BlockSpec(memory_space=pltpu.VMEM)] * 2,
        scratch_shapes=WORK
        + [
            pltpu.VMEM((8, 27, 16, 128), bf16),
            pltpu.VMEM((4, 2, 28, 16, 128), f32),
            pltpu.VMEM((4, 4, 7, 16, 128), bf16),
            pltpu.VMEM((4, 4, 7, 16, 128), bf16),
            pltpu.VMEM((3, 4, 7, 16, 128), bf16),
            pltpu.VMEM((3, 4, 7, 16, 128), bf16),
            pltpu.VMEM((4, 7, 16, 128), f32),
            pltpu.VMEM((3, 7, 16, 128), bf16),
            pltpu.VMEM((3, 7, 16, 128), bf16),
            pltpu.VMEM((7, 16, 128), f32),
            pltpu.VMEM((3, 7, 16, 128), f32),
            pltpu.VMEM((3, 8, 128), f32),
            pltpu.VMEM((7, 8, 128), f32),
            sem((3,)), sem((3,)), sem((4,)), sem((4,)),
            sem((4,)), sem((4,)), sem((3,)), sem((3,)),
            sem((3,)), sem((3,)), sem((3,)), sem((3,)),
            sem((7,)), sem((7,)),
        ],
        compiler_params=pltpu.CompilerParams(
            collective_id=1, has_side_effects=True, vmem_limit_bytes=48 * 2**20
        ),
    )(w, x, cot, bias)


def body(tiles, cotangent, weight, bias, counts):
    num_dev = lax.axis_size("dev")
    num_grp = lax.axis_size("grp")
    cap, frames, hl, wl, cin = tiles.shape
    cout = weight.shape[1]
    my_dev = lax.axis_index("dev")
    my_grp = lax.axis_index("grp")
    scale = 1.0 / math.sqrt(cap * num_dev * num_grp * frames * 4 * hl * wl)

    mine = weight.reshape(cin // num_dev, 27, cout).transpose(1, 0, 2)
    x = tiles.transpose(2, 3, 0, 1, 4).reshape(hl * wl * cap * frames, cin)
    my_count = counts[my_grp * num_dev + my_dev]
    live = (jnp.arange(cap, dtype=jnp.int32) < my_count).reshape(cap, 1, 1, 1, 1)
    cot = jnp.where(live, cotangent, jnp.zeros((), cotangent.dtype))
    cot = cot.reshape(cap, frames, hl, 2, wl, 2, cout).transpose(3, 5, 2, 4, 0, 1, 6)
    cot = cot.reshape(4, hl * wl * cap * frames, cout)

    share = cout // num_dev
    bias = bias.reshape(1, cout)
    if (num_grp, num_dev) == (4, 8):
        done, total_b = whole(mine, x, cot, bias, scale)
        done = done.reshape(28, 16, cout)
        part_w = done[:27].transpose(1, 0, 2).reshape(432, cout)
        part_b = lax.dynamic_slice_in_dim(total_b[0], my_dev * share, share, 0)
        return part_w, part_b
    gathered = lax.all_gather(mine, "dev", axis=0, tiled=False)
    if num_dev != 8:
        gathered = gathered.transpose(1, 0, 2, 3).reshape(27, 8, 16, cout)
        gathered = gathered.transpose(1, 0, 2, 3)
    parts = terms(gathered, x, cot, bias)
    flat = parts[:, :27].transpose(0, 2, 1, 3).reshape(cin * 27, cout)
    part_w = lax.psum_scatter(flat, "dev", scatter_dimension=0, tiled=True)
    part_w = lax.psum(part_w, "grp")
    total_b = lax.psum(parts[0, 27, 0], ("grp", "dev"))
    part_b = lax.dynamic_slice_in_dim(total_b, my_dev * share, share, 0)
    return part_w * scale, part_b * scale


def solution(mesh):
    return jax.shard_map(
        body,
        mesh=mesh,
        in_specs=(
            P(("grp", "dev"), None, None, None, None),
            P(("grp", "dev"), None, None, None, None),
            P("dev", None),
            P(),
            P(),
        ),
        out_specs=(P("dev", None), P("dev")),
        check_vma=False,
    )
```

```python
import functools
import math

import jax
import jax.numpy as jnp
from jax import lax
from jax.experimental import pallas as pl
from jax.experimental.pallas import tpu as pltpu
from jax.sharding import PartitionSpec as P

MESH = pl.DeviceIdType.MESH
TAPS = {(0, 0): (0,), (0, 1): (1, 2), (1, 0): (0, 1), (1, 1): (2,)}
OFFSET = ((0, 1, 1), (0, 0, 1))


def build_windows(x_ref, f_ref, xs_ref):
    rows = x_ref.shape[0]
    slab = rows // 4
    pad = 40
    row = lax.broadcasted_iota(jnp.int32, (rows, 128), 0).astype(jnp.float32)
    frame = row - 9.0 * jnp.floor((row + 0.5) * (1.0 / 9.0))
    place = lax.broadcasted_iota(jnp.int32, (slab, 128), 0)
    xs_ref[0:slab] = jnp.zeros((slab, 1152), jnp.bfloat16)
    xs_ref[5 * slab : 6 * slab] = jnp.zeros((slab, 1152), jnp.bfloat16)
    f_ref[...] = jnp.zeros_like(f_ref)
    now = x_ref[...].astype(jnp.float32)
    f_ref[2, pad : pad + rows] = now
    back1 = jnp.where(frame < 0.5, now, f_ref[2, pad - 1 : pad - 1 + rows])
    f_ref[1, pad : pad + rows] = back1
    f_ref[0, pad : pad + rows] = jnp.where(
        frame < 1.5, back1, f_ref[2, pad - 2 : pad - 2 + rows]
    )
    for h in range(4):
        for dw in range(3):
            for kd in range(3):
                start = pad + h * slab + (dw - 1) * 36
                piece = f_ref[kd, start : start + slab]
                if dw == 0:
                    piece = jnp.where(place < 36, 0.0, piece)
                if dw == 2:
                    piece = jnp.where(place >= slab - 36, 0.0, piece)
                col = dw * 384 + kd * 128
                xs_ref[(h + 1) * slab : (h + 2) * slab, col : col + 128] = piece.astype(
                    jnp.bfloat16
                )


def combine_weights(w_ref, wz_ref):
    chans = 128
    for kd in range(3):
        tap = {}
        for kh in range(3):
            for kw in range(3):
                piece = w_ref[:, 9 * kd + 3 * kh + kw]
                tap[kh, kw] = piece.reshape(chans, chans).astype(jnp.float32)
        for ph in range(2):
            for a in range(2):
                line = [sum(tap[kh, kw] for kh in TAPS[ph, a]) for kw in range(3)]
                for pw in range(2):
                    for b in range(2):
                        both = sum(line[kw] for kw in TAPS[pw, b])
                        row = (b + pw) * 384 + kd * 128
                        col = (2 * ph + pw) * 128
                        wz_ref[a + ph, row : row + 128, col : col + 128] = both.astype(
                            jnp.bfloat16
                        )


def products(count, xs_ref, cot_ref, bias_ref, wz_ref, g_ref):
    slab = xs_ref.shape[0] // 6
    rows = 4 * slab
    row = lax.broadcasted_iota(jnp.int32, (rows, 128), 0).astype(jnp.float32)
    place = row - 36.0 * jnp.floor((row + 0.5) * (1.0 / 36.0))
    live = place < 9.0 * count.astype(jnp.float32)
    cols = ((0, 256), (0, 512), (256, 256))

    def window(dh):
        return xs_ref[dh * slab : dh * slab + rows, :]

    mid = jnp.dot(window(1), wz_ref[1], preferred_element_type=jnp.float32)
    top = jnp.dot(window(0), wz_ref[0, :, 0:256], preferred_element_type=jnp.float32)
    low = jnp.dot(window(2), wz_ref[2, :, 256:512], preferred_element_type=jnp.float32)
    parts = []
    total_b = jnp.zeros((1, 128), jnp.float32)
    for p in range(4):
        side = (top if p < 2 else low)[:, (p % 2) * 128 : (p % 2) * 128 + 128]
        z = mid[:, p * 128 : p * 128 + 128] + side + bias_ref[...]
        sig = jax.nn.sigmoid(z)
        dz = cot_ref[p].astype(jnp.float32) * sig * (1.0 + z * (1.0 - sig))
        dz = jnp.where(live, dz, 0.0).astype(jnp.bfloat16)
        total_b += jnp.sum(dz.astype(jnp.float32), axis=0, keepdims=True)
        parts.append(dz)
    dz = jnp.concatenate(parts, axis=1)
    for dh in range(3):
        start, width = cols[dh]
        g_ref[dh, :, start : start + width] = lax.dot_general(
            window(dh),
            dz[:, start : start + width],
            (((0,), (0,)), ((), ())),
            preferred_element_type=jnp.float32,
        )
    return total_b


def tap_gradient(g_ref, k, base=0, size=128):
    kd, kh, kw = k // 9, k // 3 % 3, k % 3
    total = None
    for ph in range(2):
        for pw in range(2):
            row = (OFFSET[pw][kw] + pw) * 384 + kd * 128
            col = (2 * ph + pw) * 128
            term = g_ref[
                OFFSET[ph][kh] + ph, pl.ds(base + row, size), col : col + 128
            ]
            total = term if total is None else total + term
    return total


WORK = [
    pltpu.VMEM((3, 656, 128), jnp.float32),
    pltpu.VMEM((864, 1152), jnp.bfloat16),
    pltpu.VMEM((3, 1152, 512), jnp.bfloat16),
    pltpu.VMEM((3, 1152, 512), jnp.float32),
]


def terms_kernel(
    count_ref, w_ref, x_ref, cot_ref, bias_ref, out_ref, f_ref, xs_ref, wz_ref, g_ref
):
    build_windows(x_ref, f_ref, xs_ref)
    wz_ref[...] = jnp.zeros_like(wz_ref)
    combine_weights(w_ref, wz_ref)
    total_b = products(count_ref[0], xs_ref, cot_ref, bias_ref, wz_ref, g_ref)
    for k in range(27):
        out_ref[:, k] = tap_gradient(g_ref, k).reshape(8, 16, 128)
    out_ref[:, 27] = jnp.broadcast_to(total_b.reshape(1, 1, 128), (8, 16, 128))


def terms(count, w, x, cot, bias):
    return pl.pallas_call(
        terms_kernel,
        out_shape=jax.ShapeDtypeStruct((8, 28, 16, 128), jnp.float32),
        in_specs=[pl.BlockSpec(memory_space=pltpu.SMEM)]
        + [pl.BlockSpec(memory_space=pltpu.VMEM)] * 4,
        out_specs=pl.BlockSpec(memory_space=pltpu.VMEM),
        scratch_shapes=WORK,
        compiler_params=pltpu.CompilerParams(vmem_limit_bytes=48 * 2**20),
    )(count, w, x, cot, bias)


def whole_kernel(
    scale, counts_ref, w_ref, x_ref, cot_ref, bias_ref, o_ref, b_ref,
    f_ref, xs_ref, wz_ref, g_ref, w_all, parts,
    s1, r1, s2, r2, keep, s3, r3, s4, r4, sb, rb,
    sw1, rw1, sw2, rw2, ss1, rs1, ss2, rs2, ss3, rs3, ss4, rs4, ssb, rsb,
):
    grp = lax.axis_index("grp")
    dev = lax.axis_index("dev")
    depth = dev // 2
    core = dev % 2
    f32, bf16 = jnp.float32, jnp.bfloat16
    pair = {"dev": depth * 2 + (1 - core)}
    across = [{"grp": (grp + k) % 4} for k in range(1, 4)]
    along = [{"dev": ((depth + k) % 4) * 2 + core} for k in range(1, 4)]

    barrier = pltpu.get_barrier_semaphore()
    for peer in [pair] + across + along:
        pl.semaphore_signal(barrier, inc=1, device_id=peer, device_id_type=MESH)
    pl.semaphore_wait(barrier, 7)

    def send(src, dst, ssem, rsem, peer):
        copy = pltpu.make_async_remote_copy(
            src_ref=src, dst_ref=dst, send_sem=ssem, recv_sem=rsem,
            device_id=peer, device_id_type=MESH,
        )
        copy.start()
        return copy

    out = [
        send(w_ref, w_all.at[dev], sw1.at[k], rw1.at[k], along[k]) for k in range(3)
    ]
    swap = [send(w_ref, w_all.at[dev], sw2.at[3], rw2.at[3], pair)]
    w_all[dev] = w_ref[...]
    wz_ref[...] = jnp.zeros_like(wz_ref)
    build_windows(x_ref, f_ref, xs_ref)
    for k in (0, 2, 1):
        out[k].wait_recv()
        block = w_all.at[((depth + 3 - k) % 4) * 2 + core]
        swap.append(send(block, block, sw2.at[k], rw2.at[k], pair))
    for copy in swap:
        copy.wait_recv()
    combine_weights(w_all, wz_ref)
    total_b = products(counts_ref[grp * 8 + dev], xs_ref, cot_ref, bias_ref, wz_ref, g_ref)

    sb[0] = jnp.broadcast_to(total_b, (8, 128))
    bias_copies = [send(sb.at[0], rb.at[0], ssb.at[0], rsb.at[0], pair)]
    first, second, third = [], [], []

    def start_first(k):
        base = pl.multiple_of(((depth + k + 1) % 4) * 32, 32)
        for tap in range(27):
            parts[k, :, tap] = tap_gradient(g_ref, tap, base, 32).reshape(2, 16, 128)
        parts[k, :, 27] = jnp.zeros((2, 16, 128), f32)
        s1[k] = parts[k, 1 - core].astype(bf16)
        first.append(send(s1.at[k], r1.at[k], ss1.at[k], rs1.at[k], pair))

    def start_second(k):
        first[k].wait_recv()
        for j in range(4):
            taps = pl.ds(((grp + j + 1) % 4) * 7, 7)
            total = parts[k, core, taps] + r1[k, taps].astype(f32)
            if j < 3:
                s2[k, j] = total.astype(bf16)
                second.append(
                    send(
                        s2.at[k, j], r2.at[k, j], ss2.at[k, j], rs2.at[k, j], across[j]
                    )
                )
            else:
                keep[k] = total

    def start_third(k):
        total = keep[k]
        for j in range(3):
            second[3 * k + j].wait_recv()
            total += r2[k, j].astype(f32)
        if k < 3:
            s3[k] = total.astype(bf16)
            third.append(send(s3.at[k], r3.at[k], ss3.at[k], rs3.at[k], along[k]))
        else:
            keep[k] = total

    start_first(0)
    start_first(1)
    start_second(0)
    start_first(2)
    bias_copies[0].wait_recv()
    sb[1] = sb[0] + rb[0]
    for k in range(3):
        bias_copies.append(
            send(sb.at[1], rb.at[1 + k], ssb.at[1 + k], rsb.at[1 + k], across[k])
        )
    start_second(1)
    start_first(3)
    start_second(2)
    start_third(0)
    start_second(3)
    start_third(1)
    for k in range(3):
        bias_copies[1 + k].wait_recv()
    sb[2] = (sb[1] + rb[1]) + (rb[2] + rb[3])
    for k in range(3):
        bias_copies.append(
            send(sb.at[2], rb.at[4 + k], ssb.at[4 + k], rsb.at[4 + k], along[k])
        )
    start_third(2)
    start_third(3)
    for k in range(3):
        bias_copies[4 + k].wait_recv()
    b_ref[...] = ((sb[2] + rb[4]) + (rb[5] + rb[6])) * scale
    total = keep[3]
    for k in range(3):
        third[k].wait_recv()
        total += r3[k].astype(f32)
    total = total * scale
    s4[...] = total
    fourth = [
        send(s4, r4.at[k], ss4.at[k], rs4.at[k], across[k]) for k in range(3)
    ]
    o_ref[grp] = total
    for k in range(3):
        fourth[k].wait_recv()
        o_ref[(grp + 3 - k) % 4] = r4[k]
    for copy in out + swap + bias_copies + first + second + third + fourth:
        copy.wait_send()


def whole(counts, w, x, cot, bias, scale):
    bf16, f32 = jnp.bfloat16, jnp.float32
    sem = pltpu.SemaphoreType.DMA
    return pl.pallas_call(
        functools.partial(whole_kernel, scale),
        out_shape=(
            jax.ShapeDtypeStruct((4, 7, 16, 128), f32),
            jax.ShapeDtypeStruct((8, 128), f32),
        ),
        in_specs=[pl.BlockSpec(memory_space=pltpu.SMEM)]
        + [pl.BlockSpec(memory_space=pltpu.VMEM)] * 4,
        out_specs=[pl.BlockSpec(memory_space=pltpu.VMEM)] * 2,
        scratch_shapes=WORK
        + [
            pltpu.VMEM((8, 27, 16, 128), bf16),
            pltpu.VMEM((4, 2, 28, 16, 128), f32),
            pltpu.VMEM((4, 28, 16, 128), bf16),
            pltpu.VMEM((4, 28, 16, 128), bf16),
            pltpu.VMEM((4, 3, 7, 16, 128), bf16),
            pltpu.VMEM((4, 3, 7, 16, 128), bf16),
            pltpu.VMEM((4, 7, 16, 128), f32),
            pltpu.VMEM((3, 7, 16, 128), bf16),
            pltpu.VMEM((3, 7, 16, 128), bf16),
            pltpu.VMEM((7, 16, 128), f32),
            pltpu.VMEM((3, 7, 16, 128), f32),
            pltpu.VMEM((3, 8, 128), f32),
            pltpu.VMEM((7, 8, 128), f32),
            sem((3,)), sem((3,)), sem((4,)), sem((4,)),
            sem((4,)), sem((4,)), sem((4, 3)), sem((4, 3)),
            sem((3,)), sem((3,)), sem((3,)), sem((3,)),
            sem((7,)), sem((7,)),
        ],
        compiler_params=pltpu.CompilerParams(
            collective_id=1, has_side_effects=True, vmem_limit_bytes=48 * 2**20
        ),
    )(counts, w, x, cot, bias)


def body(tiles, cotangent, weight, bias, counts):
    num_dev = lax.axis_size("dev")
    num_grp = lax.axis_size("grp")
    cap, frames, hl, wl, cin = tiles.shape
    cout = weight.shape[1]
    my_dev = lax.axis_index("dev")
    my_grp = lax.axis_index("grp")
    scale = 1.0 / math.sqrt(cap * num_dev * num_grp * frames * 4 * hl * wl)

    mine = weight.reshape(cin // num_dev, 27, cout).transpose(1, 0, 2)
    x = tiles.transpose(2, 3, 0, 1, 4).reshape(hl * wl * cap * frames, cin)
    cot = cotangent.reshape(cap, frames, hl, 2, wl, 2, cout).transpose(3, 5, 2, 4, 0, 1, 6)
    cot = cot.reshape(4, hl * wl * cap * frames, cout)

    share = cout // num_dev
    bias = bias.reshape(1, cout)
    if (num_grp, num_dev) == (4, 8):
        done, total_b = whole(counts, mine, x, cot, bias, scale)
        done = done.reshape(28, 16, cout)
        part_w = done[:27].transpose(1, 0, 2).reshape(432, cout)
        part_b = lax.dynamic_slice_in_dim(total_b[0], my_dev * share, share, 0)
        return part_w, part_b
    gathered = lax.all_gather(mine, "dev", axis=0, tiled=False)
    if num_dev != 8:
        gathered = gathered.transpose(1, 0, 2, 3).reshape(27, 8, 16, cout)
        gathered = gathered.transpose(1, 0, 2, 3)
    count = lax.dynamic_slice_in_dim(counts, my_grp * num_dev + my_dev, 1)
    parts = terms(count, gathered, x, cot, bias)
    flat = parts[:, :27].transpose(0, 2, 1, 3).reshape(cin * 27, cout)
    part_w = lax.psum_scatter(flat, "dev", scatter_dimension=0, tiled=True)
    part_w = lax.psum(part_w, "grp")
    total_b = lax.psum(parts[0, 27, 0], ("grp", "dev"))
    part_b = lax.dynamic_slice_in_dim(total_b, my_dev * share, share, 0)
    return part_w * scale, part_b * scale


def solution(mesh):
    return jax.shard_map(
        body,
        mesh=mesh,
        in_specs=(
            P(("grp", "dev"), None, None, None, None),
            P(("grp", "dev"), None, None, None, None),
            P("dev", None),
            P(),
            P(),
        ),
        out_specs=(P("dev", None), P("dev")),
        check_vma=False,
    )
```

```python
import functools
import math

import jax
import jax.numpy as jnp
from jax import lax
from jax.experimental import pallas as pl
from jax.experimental.pallas import tpu as pltpu
from jax.sharding import PartitionSpec as P

MESH = pl.DeviceIdType.MESH
TAPS = {(0, 0): (0,), (0, 1): (1, 2), (1, 0): (0, 1), (1, 1): (2,)}
OFFSET = ((0, 1, 1), (0, 0, 1))


def build_windows(x_ref, f_ref, xs_ref):
    rows = x_ref.shape[0]
    slab = rows // 4
    pad = 40
    row = lax.broadcasted_iota(jnp.int32, (rows, 128), 0).astype(jnp.float32)
    frame = row - 9.0 * jnp.floor((row + 0.5) * (1.0 / 9.0))
    place = lax.broadcasted_iota(jnp.int32, (slab, 128), 0)
    xs_ref[0:slab] = jnp.zeros((slab, 1152), jnp.bfloat16)
    xs_ref[5 * slab : 6 * slab] = jnp.zeros((slab, 1152), jnp.bfloat16)
    f_ref[...] = jnp.zeros_like(f_ref)
    now = x_ref[...].astype(jnp.float32)
    f_ref[2, pad : pad + rows] = now
    back1 = jnp.where(frame < 0.5, now, f_ref[2, pad - 1 : pad - 1 + rows])
    f_ref[1, pad : pad + rows] = back1
    f_ref[0, pad : pad + rows] = jnp.where(
        frame < 1.5, back1, f_ref[2, pad - 2 : pad - 2 + rows]
    )
    for h in range(4):
        for dw in range(3):
            for kd in range(3):
                start = pad + h * slab + (dw - 1) * 36
                piece = f_ref[kd, start : start + slab]
                if dw == 0:
                    piece = jnp.where(place < 36, 0.0, piece)
                if dw == 2:
                    piece = jnp.where(place >= slab - 36, 0.0, piece)
                col = dw * 384 + kd * 128
                xs_ref[(h + 1) * slab : (h + 2) * slab, col : col + 128] = piece.astype(
                    jnp.bfloat16
                )


def combine_weights(w_ref, wz_ref):
    chans = 128
    for kd in range(3):
        tap = {}
        for kh in range(3):
            for kw in range(3):
                piece = w_ref[:, 9 * kd + 3 * kh + kw]
                tap[kh, kw] = piece.reshape(chans, chans).astype(jnp.float32)
        for ph in range(2):
            for a in range(2):
                line = [sum(tap[kh, kw] for kh in TAPS[ph, a]) for kw in range(3)]
                for pw in range(2):
                    for b in range(2):
                        both = sum(line[kw] for kw in TAPS[pw, b])
                        row = (b + pw) * 384 + kd * 128
                        col = (2 * ph + pw) * 128
                        wz_ref[a + ph, row : row + 128, col : col + 128] = both.astype(
                            jnp.bfloat16
                        )


def products(count, xs_ref, cot_ref, bias_ref, wz_ref, g_ref):
    slab = xs_ref.shape[0] // 6
    rows = 4 * slab
    row = lax.broadcasted_iota(jnp.int32, (rows, 128), 0).astype(jnp.float32)
    place = row - 36.0 * jnp.floor((row + 0.5) * (1.0 / 36.0))
    live = place < 9.0 * count.astype(jnp.float32)
    cols = ((0, 256), (0, 512), (256, 256))

    def window(dh):
        return xs_ref[dh * slab : dh * slab + rows, :]

    mid = jnp.dot(window(1), wz_ref[1], preferred_element_type=jnp.float32)
    top = jnp.dot(window(0), wz_ref[0, :, 0:256], preferred_element_type=jnp.float32)
    low = jnp.dot(window(2), wz_ref[2, :, 256:512], preferred_element_type=jnp.float32)
    parts = []
    total_b = jnp.zeros((1, 128), jnp.float32)
    for p in range(4):
        side = (top if p < 2 else low)[:, (p % 2) * 128 : (p % 2) * 128 + 128]
        z = mid[:, p * 128 : p * 128 + 128] + side + bias_ref[...]
        sig = jax.nn.sigmoid(z)
        dz = cot_ref[p].astype(jnp.float32) * sig * (1.0 + z * (1.0 - sig))
        dz = jnp.where(live, dz, 0.0).astype(jnp.bfloat16)
        total_b += jnp.sum(dz.astype(jnp.float32), axis=0, keepdims=True)
        parts.append(dz)
    dz = jnp.concatenate(parts, axis=1)
    for dh in range(3):
        start, width = cols[dh]
        g_ref[dh, :, start : start + width] = lax.dot_general(
            window(dh),
            dz[:, start : start + width],
            (((0,), (0,)), ((), ())),
            preferred_element_type=jnp.float32,
        )
    return total_b


def tap_gradient(g_ref, k, base=0, size=128):
    kd, kh, kw = k // 9, k // 3 % 3, k % 3
    total = None
    for ph in range(2):
        for pw in range(2):
            row = (OFFSET[pw][kw] + pw) * 384 + kd * 128
            col = (2 * ph + pw) * 128
            term = g_ref[
                OFFSET[ph][kh] + ph, pl.ds(base + row, size), col : col + 128
            ]
            total = term if total is None else total + term
    return total


WORK = [
    pltpu.VMEM((3, 656, 128), jnp.float32),
    pltpu.VMEM((864, 1152), jnp.bfloat16),
    pltpu.VMEM((3, 1152, 512), jnp.bfloat16),
    pltpu.VMEM((3, 1152, 512), jnp.float32),
]


def terms_kernel(
    count_ref, w_ref, x_ref, cot_ref, bias_ref, out_ref, f_ref, xs_ref, wz_ref, g_ref
):
    build_windows(x_ref, f_ref, xs_ref)
    wz_ref[...] = jnp.zeros_like(wz_ref)
    combine_weights(w_ref, wz_ref)
    total_b = products(count_ref[0], xs_ref, cot_ref, bias_ref, wz_ref, g_ref)
    for k in range(27):
        out_ref[:, k] = tap_gradient(g_ref, k).reshape(8, 16, 128)
    out_ref[:, 27] = jnp.broadcast_to(total_b.reshape(1, 1, 128), (8, 16, 128))


def terms(count, w, x, cot, bias):
    return pl.pallas_call(
        terms_kernel,
        out_shape=jax.ShapeDtypeStruct((8, 28, 16, 128), jnp.float32),
        in_specs=[pl.BlockSpec(memory_space=pltpu.SMEM)]
        + [pl.BlockSpec(memory_space=pltpu.VMEM)] * 4,
        out_specs=pl.BlockSpec(memory_space=pltpu.VMEM),
        scratch_shapes=WORK,
        compiler_params=pltpu.CompilerParams(vmem_limit_bytes=48 * 2**20),
    )(count, w, x, cot, bias)


def whole_kernel(
    scale, counts_ref, w_ref, x_ref, cot_any, bias_ref, o_ref, b_ref,
    f_ref, xs_ref, wz_ref, g_ref, w_all, parts,
    s1, r1, s2, r2, keep, s3, r3, s4, r4, sb, rb,
    cot_ref, fetch_sem, sw3, rw3, sw1, rw1, sw2, rw2, ss1, rs1, ss2, rs2, ss3, rs3, ss4, rs4, ssb, rsb,
):
    grp = lax.axis_index("grp")
    dev = lax.axis_index("dev")
    depth = dev // 2
    core = dev % 2
    f32, bf16 = jnp.float32, jnp.bfloat16
    pair = {"dev": depth * 2 + (1 - core)}
    across = [{"grp": (grp + k) % 4} for k in range(1, 4)]
    along = [{"dev": ((depth + k) % 4) * 2 + core} for k in range(1, 4)]

    barrier = pltpu.get_barrier_semaphore()
    for peer in [pair] + across + along:
        pl.semaphore_signal(barrier, inc=1, device_id=peer, device_id_type=MESH)
    pl.semaphore_wait(barrier, 7)

    def send(src, dst, ssem, rsem, peer):
        copy = pltpu.make_async_remote_copy(
            src_ref=src, dst_ref=dst, send_sem=ssem, recv_sem=rsem,
            device_id=peer, device_id_type=MESH,
        )
        copy.start()
        return copy

    fetch = pltpu.make_async_copy(cot_any, cot_ref, fetch_sem)
    fetch.start()
    quarter = pl.ds(grp * 7, 7)
    out = [
        send(
            w_ref.at[quarter], w_all.at[dev, quarter], sw1.at[k], rw1.at[k], along[k]
        )
        for k in (0, 2, 1)
    ]
    swap = [send(w_ref, w_all.at[dev], sw2.at[3], rw2.at[3], pair)]
    w_all[dev] = w_ref[...]
    wz_ref[...] = jnp.zeros_like(wz_ref)
    spread = []
    for i, k in enumerate((0, 2, 1)):
        out[i].wait_recv()
        block = w_all.at[((depth + 3 - k) % 4) * 2 + core, quarter]
        for j in range(3):
            spread.append(
                send(block, block, sw3.at[k, j], rw3.at[k, j], across[j])
            )
    build_windows(x_ref, f_ref, xs_ref)
    for i, k in enumerate((0, 2, 1)):
        for j in range(3):
            spread[3 * i + j].wait_recv()
        block = w_all.at[((depth + 3 - k) % 4) * 2 + core]
        swap.append(send(block, block, sw2.at[k], rw2.at[k], pair))
    for copy in swap:
        copy.wait_recv()
    combine_weights(w_all, wz_ref)
    fetch.wait()
    total_b = products(counts_ref[grp * 8 + dev], xs_ref, cot_ref, bias_ref, wz_ref, g_ref)

    sb[0] = jnp.broadcast_to(total_b, (8, 128))
    bias_copies = [send(sb.at[0], rb.at[0], ssb.at[0], rsb.at[0], pair)]
    first, second, third = [], [], []

    def start_first(k):
        base = pl.multiple_of(((depth + k + 1) % 4) * 32, 32)
        for tap in range(27):
            parts[k, :, tap] = tap_gradient(g_ref, tap, base, 32).reshape(2, 16, 128)
        parts[k, :, 27] = jnp.zeros((2, 16, 128), f32)
        s1[k] = parts[k, 1 - core].astype(bf16)
        first.append(send(s1.at[k], r1.at[k], ss1.at[k], rs1.at[k], pair))

    def start_second(k):
        first[k].wait_recv()
        for j in range(4):
            taps = pl.ds(((grp + j + 1) % 4) * 7, 7)
            total = parts[k, core, taps] + r1[k, taps].astype(f32)
            if j < 3:
                s2[k, j] = total.astype(bf16)
                second.append(
                    send(
                        s2.at[k, j], r2.at[k, j], ss2.at[k, j], rs2.at[k, j], across[j]
                    )
                )
            else:
                keep[k] = total

    def start_third(k):
        total = keep[k]
        for j in range(3):
            second[3 * k + j].wait_recv()
            total += r2[k, j].astype(f32)
        if k < 3:
            s3[k] = total.astype(bf16)
            third.append(send(s3.at[k], r3.at[k], ss3.at[k], rs3.at[k], along[k]))
        else:
            keep[k] = total

    start_first(0)
    start_first(1)
    start_second(0)
    start_first(2)
    bias_copies[0].wait_recv()
    sb[1] = sb[0] + rb[0]
    for k in range(3):
        bias_copies.append(
            send(sb.at[1], rb.at[1 + k], ssb.at[1 + k], rsb.at[1 + k], across[k])
        )
    start_second(1)
    start_first(3)
    start_second(2)
    start_third(0)
    start_second(3)
    start_third(1)
    for k in range(3):
        bias_copies[1 + k].wait_recv()
    sb[2] = (sb[1] + rb[1]) + (rb[2] + rb[3])
    for k in range(3):
        bias_copies.append(
            send(sb.at[2], rb.at[4 + k], ssb.at[4 + k], rsb.at[4 + k], along[k])
        )
    start_third(2)
    start_third(3)
    for k in range(3):
        bias_copies[4 + k].wait_recv()
    b_ref[...] = ((sb[2] + rb[4]) + (rb[5] + rb[6])) * scale
    total = keep[3]
    for k in range(3):
        third[k].wait_recv()
        total += r3[k].astype(f32)
    total = total * scale
    s4[...] = total
    fourth = [
        send(s4, r4.at[k], ss4.at[k], rs4.at[k], across[k]) for k in range(3)
    ]
    o_ref[grp] = total
    for k in range(3):
        fourth[k].wait_recv()
        o_ref[(grp + 3 - k) % 4] = r4[k]
    for copy in out + spread + swap + bias_copies + first + second + third + fourth:
        copy.wait_send()


def whole(counts, w, x, cot, bias, scale):
    bf16, f32 = jnp.bfloat16, jnp.float32
    sem = pltpu.SemaphoreType.DMA
    return pl.pallas_call(
        functools.partial(whole_kernel, scale),
        out_shape=(
            jax.ShapeDtypeStruct((4, 7, 16, 128), f32),
            jax.ShapeDtypeStruct((8, 128), f32),
        ),
        in_specs=[pl.BlockSpec(memory_space=pltpu.SMEM)]
        + [pl.BlockSpec(memory_space=pltpu.VMEM)] * 2
        + [pl.BlockSpec(memory_space=pl.ANY)]
        + [pl.BlockSpec(memory_space=pltpu.VMEM)],
        out_specs=[pl.BlockSpec(memory_space=pltpu.VMEM)] * 2,
        scratch_shapes=WORK
        + [
            pltpu.VMEM((8, 28, 16, 128), bf16),
            pltpu.VMEM((4, 2, 28, 16, 128), f32),
            pltpu.VMEM((4, 28, 16, 128), bf16),
            pltpu.VMEM((4, 28, 16, 128), bf16),
            pltpu.VMEM((4, 3, 7, 16, 128), bf16),
            pltpu.VMEM((4, 3, 7, 16, 128), bf16),
            pltpu.VMEM((4, 7, 16, 128), f32),
            pltpu.VMEM((3, 7, 16, 128), bf16),
            pltpu.VMEM((3, 7, 16, 128), bf16),
            pltpu.VMEM((7, 16, 128), f32),
            pltpu.VMEM((3, 7, 16, 128), f32),
            pltpu.VMEM((3, 8, 128), f32),
            pltpu.VMEM((7, 8, 128), f32),
            pltpu.VMEM((4, 576, 128), bf16),
            sem, sem((3, 3)), sem((3, 3)),
            sem((3,)), sem((3,)), sem((4,)), sem((4,)),
            sem((4,)), sem((4,)), sem((4, 3)), sem((4, 3)),
            sem((3,)), sem((3,)), sem((3,)), sem((3,)),
            sem((7,)), sem((7,)),
        ],
        compiler_params=pltpu.CompilerParams(
            collective_id=1, has_side_effects=True, vmem_limit_bytes=48 * 2**20
        ),
    )(counts, w, x, cot, bias)


def body(tiles, cotangent, weight, bias, counts):
    num_dev = lax.axis_size("dev")
    num_grp = lax.axis_size("grp")
    cap, frames, hl, wl, cin = tiles.shape
    cout = weight.shape[1]
    my_dev = lax.axis_index("dev")
    my_grp = lax.axis_index("grp")
    scale = 1.0 / math.sqrt(cap * num_dev * num_grp * frames * 4 * hl * wl)

    mine = weight.reshape(cin // num_dev, 27, cout).transpose(1, 0, 2)
    x = tiles.transpose(2, 3, 0, 1, 4).reshape(hl * wl * cap * frames, cin)
    cot = cotangent.reshape(cap, frames, hl, 2, wl, 2, cout).transpose(3, 5, 2, 4, 0, 1, 6)
    cot = cot.reshape(4, hl * wl * cap * frames, cout)

    share = cout // num_dev
    bias = bias.reshape(1, cout)
    if (num_grp, num_dev) == (4, 8):
        mine = jnp.pad(mine, ((0, 1), (0, 0), (0, 0)))
        done, total_b = whole(counts, mine, x, cot, bias, scale)
        done = done.reshape(28, 16, cout)
        part_w = done[:27].transpose(1, 0, 2).reshape(432, cout)
        part_b = lax.dynamic_slice_in_dim(total_b[0], my_dev * share, share, 0)
        return part_w, part_b
    gathered = lax.all_gather(mine, "dev", axis=0, tiled=False)
    if num_dev != 8:
        gathered = gathered.transpose(1, 0, 2, 3).reshape(27, 8, 16, cout)
        gathered = gathered.transpose(1, 0, 2, 3)
    count = lax.dynamic_slice_in_dim(counts, my_grp * num_dev + my_dev, 1)
    parts = terms(count, gathered, x, cot, bias)
    flat = parts[:, :27].transpose(0, 2, 1, 3).reshape(cin * 27, cout)
    part_w = lax.psum_scatter(flat, "dev", scatter_dimension=0, tiled=True)
    part_w = lax.psum(part_w, "grp")
    total_b = lax.psum(parts[0, 27, 0], ("grp", "dev"))
    part_b = lax.dynamic_slice_in_dim(total_b, my_dev * share, share, 0)
    return part_w * scale, part_b * scale


def solution(mesh):
    return jax.shard_map(
        body,
        mesh=mesh,
        in_specs=(
            P(("grp", "dev"), None, None, None, None),
            P(("grp", "dev"), None, None, None, None),
            P("dev", None),
            P(),
            P(),
        ),
        out_specs=(P("dev", None), P("dev")),
        check_vma=False,
    )
```

```python
import functools
import math

import jax
import jax.numpy as jnp
from jax import lax
from jax.experimental import pallas as pl
from jax.experimental.pallas import tpu as pltpu
from jax.sharding import PartitionSpec as P

MESH = pl.DeviceIdType.MESH
TAPS = {(0, 0): (0,), (0, 1): (1, 2), (1, 0): (0, 1), (1, 1): (2,)}
OFFSET = ((0, 1, 1), (0, 0, 1))


def build_windows(x_ref, f_ref, xs_ref):
    rows = x_ref.shape[0]
    slab = rows // 4
    pad = 40
    row = lax.broadcasted_iota(jnp.int32, (rows, 128), 0).astype(jnp.float32)
    frame = row - 9.0 * jnp.floor((row + 0.5) * (1.0 / 9.0))
    place = lax.broadcasted_iota(jnp.int32, (slab, 128), 0)
    xs_ref[0:slab] = jnp.zeros((slab, 1152), jnp.bfloat16)
    xs_ref[5 * slab : 6 * slab] = jnp.zeros((slab, 1152), jnp.bfloat16)
    f_ref[...] = jnp.zeros_like(f_ref)
    now = x_ref[...].astype(jnp.float32)
    f_ref[2, pad : pad + rows] = now
    back1 = jnp.where(frame < 0.5, now, f_ref[2, pad - 1 : pad - 1 + rows])
    f_ref[1, pad : pad + rows] = back1
    f_ref[0, pad : pad + rows] = jnp.where(
        frame < 1.5, back1, f_ref[2, pad - 2 : pad - 2 + rows]
    )
    for h in range(4):
        for dw in range(3):
            for kd in range(3):
                start = pad + h * slab + (dw - 1) * 36
                piece = f_ref[kd, start : start + slab]
                if dw == 0:
                    piece = jnp.where(place < 36, 0.0, piece)
                if dw == 2:
                    piece = jnp.where(place >= slab - 36, 0.0, piece)
                col = dw * 384 + kd * 128
                xs_ref[(h + 1) * slab : (h + 2) * slab, col : col + 128] = piece.astype(
                    jnp.bfloat16
                )


def combine_weights(w_ref, wz_ref):
    chans = 128
    for kd in range(3):
        tap = {}
        for kh in range(3):
            for kw in range(3):
                piece = w_ref[:, 9 * kd + 3 * kh + kw]
                tap[kh, kw] = piece.reshape(chans, chans).astype(jnp.float32)
        for ph in range(2):
            for a in range(2):
                line = [sum(tap[kh, kw] for kh in TAPS[ph, a]) for kw in range(3)]
                for pw in range(2):
                    for b in range(2):
                        both = sum(line[kw] for kw in TAPS[pw, b])
                        row = (b + pw) * 384 + kd * 128
                        col = (2 * ph + pw) * 128
                        wz_ref[a + ph, row : row + 128, col : col + 128] = both.astype(
                            jnp.bfloat16
                        )


def products(count, xs_ref, cot_ref, bias_ref, wz_ref, g_ref):
    slab = xs_ref.shape[0] // 6
    rows = 4 * slab
    row = lax.broadcasted_iota(jnp.int32, (rows, 128), 0).astype(jnp.float32)
    place = row - 36.0 * jnp.floor((row + 0.5) * (1.0 / 36.0))
    live = place < 9.0 * count.astype(jnp.float32)
    cols = ((0, 256), (0, 512), (256, 256))

    def window(dh):
        return xs_ref[dh * slab : dh * slab + rows, :]

    mid = jnp.dot(window(1), wz_ref[1], preferred_element_type=jnp.float32)
    top = jnp.dot(window(0), wz_ref[0, :, 0:256], preferred_element_type=jnp.float32)
    low = jnp.dot(window(2), wz_ref[2, :, 256:512], preferred_element_type=jnp.float32)
    parts = []
    total_b = jnp.zeros((1, 128), jnp.float32)
    for p in range(4):
        side = (top if p < 2 else low)[:, (p % 2) * 128 : (p % 2) * 128 + 128]
        z = mid[:, p * 128 : p * 128 + 128] + side + bias_ref[...]
        sig = jax.nn.sigmoid(z)
        dz = cot_ref[p].astype(jnp.float32) * sig * (1.0 + z * (1.0 - sig))
        dz = jnp.where(live, dz, 0.0).astype(jnp.bfloat16)
        total_b += jnp.sum(dz.astype(jnp.float32), axis=0, keepdims=True)
        parts.append(dz)
    dz = jnp.concatenate(parts, axis=1)
    for dh in range(3):
        start, width = cols[dh]
        g_ref[dh, :, start : start + width] = lax.dot_general(
            window(dh),
            dz[:, start : start + width],
            (((0,), (0,)), ((), ())),
            preferred_element_type=jnp.float32,
        )
    return total_b


def tap_gradient(g_ref, k, base=0, size=128):
    kd, kh, kw = k // 9, k // 3 % 3, k % 3
    total = None
    for ph in range(2):
        for pw in range(2):
            row = (OFFSET[pw][kw] + pw) * 384 + kd * 128
            col = (2 * ph + pw) * 128
            term = g_ref[
                OFFSET[ph][kh] + ph, pl.ds(base + row, size), col : col + 128
            ]
            total = term if total is None else total + term
    return total


WORK = [
    pltpu.VMEM((3, 656, 128), jnp.float32),
    pltpu.VMEM((864, 1152), jnp.bfloat16),
    pltpu.VMEM((3, 1152, 512), jnp.bfloat16),
    pltpu.VMEM((3, 1152, 512), jnp.float32),
]


def terms_kernel(
    count_ref, w_ref, x_ref, cot_ref, bias_ref, out_ref, f_ref, xs_ref, wz_ref, g_ref
):
    build_windows(x_ref, f_ref, xs_ref)
    wz_ref[...] = jnp.zeros_like(wz_ref)
    combine_weights(w_ref, wz_ref)
    total_b = products(count_ref[0], xs_ref, cot_ref, bias_ref, wz_ref, g_ref)
    for k in range(27):
        out_ref[:, k] = tap_gradient(g_ref, k).reshape(8, 16, 128)
    out_ref[:, 27] = jnp.broadcast_to(total_b.reshape(1, 1, 128), (8, 16, 128))


def terms(count, w, x, cot, bias):
    return pl.pallas_call(
        terms_kernel,
        out_shape=jax.ShapeDtypeStruct((8, 28, 16, 128), jnp.float32),
        in_specs=[pl.BlockSpec(memory_space=pltpu.SMEM)]
        + [pl.BlockSpec(memory_space=pltpu.VMEM)] * 4,
        out_specs=pl.BlockSpec(memory_space=pltpu.VMEM),
        scratch_shapes=WORK,
        compiler_params=pltpu.CompilerParams(vmem_limit_bytes=48 * 2**20),
    )(count, w, x, cot, bias)


def whole_kernel(
    scale, counts_ref, w_ref, x_any, cot_any, bias_ref, o_ref, b_ref,
    f_ref, xs_ref, wz_ref, g_ref, w_all, parts,
    s1, r1, s2, r2, keep, s3, r3, s4, r4, sb, rb,
    cot_ref, fetch_sem, x_ref, x_sem, sw3, rw3, sw1, rw1, sw2, rw2, ss1, rs1, ss2, rs2, ss3, rs3, ss4, rs4, ssb, rsb,
):
    grp = lax.axis_index("grp")
    dev = lax.axis_index("dev")
    depth = dev // 2
    core = dev % 2
    f32, bf16 = jnp.float32, jnp.bfloat16
    pair = {"dev": depth * 2 + (1 - core)}
    across = [{"grp": (grp + k) % 4} for k in range(1, 4)]
    along = [{"dev": ((depth + k) % 4) * 2 + core} for k in range(1, 4)]

    fetch_x = pltpu.make_async_copy(x_any, x_ref, x_sem)
    fetch_x.start()
    fetch = pltpu.make_async_copy(cot_any, cot_ref, fetch_sem)
    fetch.start()
    barrier = pltpu.get_barrier_semaphore()
    for peer in [pair] + across + along:
        pl.semaphore_signal(barrier, inc=1, device_id=peer, device_id_type=MESH)
    pl.semaphore_wait(barrier, 7)

    def send(src, dst, ssem, rsem, peer):
        copy = pltpu.make_async_remote_copy(
            src_ref=src, dst_ref=dst, send_sem=ssem, recv_sem=rsem,
            device_id=peer, device_id_type=MESH,
        )
        copy.start()
        return copy

    quarter = pl.ds(grp * 7, 7)
    out = [
        send(
            w_ref.at[quarter], w_all.at[dev, quarter], sw1.at[k], rw1.at[k], along[k]
        )
        for k in (0, 2, 1)
    ]
    swap = [send(w_ref, w_all.at[dev], sw2.at[3], rw2.at[3], pair)]
    w_all[dev] = w_ref[...]
    wz_ref[...] = jnp.zeros_like(wz_ref)
    spread = []
    for i, k in enumerate((0, 2, 1)):
        out[i].wait_recv()
        block = w_all.at[((depth + 3 - k) % 4) * 2 + core, quarter]
        for j in range(3):
            spread.append(
                send(block, block, sw3.at[k, j], rw3.at[k, j], across[j])
            )
    fetch_x.wait()
    build_windows(x_ref, f_ref, xs_ref)
    for i, k in enumerate((0, 2, 1)):
        for j in range(3):
            spread[3 * i + j].wait_recv()
        block = w_all.at[((depth + 3 - k) % 4) * 2 + core]
        swap.append(send(block, block, sw2.at[k], rw2.at[k], pair))
    for copy in swap:
        copy.wait_recv()
    combine_weights(w_all, wz_ref)
    fetch.wait()
    total_b = products(counts_ref[grp * 8 + dev], xs_ref, cot_ref, bias_ref, wz_ref, g_ref)

    sb[0] = jnp.broadcast_to(total_b, (8, 128))
    bias_copies = [send(sb.at[0], rb.at[0], ssb.at[0], rsb.at[0], pair)]
    first, second, third = [], [], []

    def start_first(k):
        base = pl.multiple_of(((depth + k + 1) % 4) * 32, 32)
        for tap in range(27):
            parts[k, :, tap] = tap_gradient(g_ref, tap, base, 32).reshape(2, 16, 128)
        parts[k, :, 27] = jnp.zeros((2, 16, 128), f32)
        s1[k] = parts[k, 1 - core].astype(bf16)
        first.append(send(s1.at[k], r1.at[k], ss1.at[k], rs1.at[k], pair))

    def start_second(k):
        first[k].wait_recv()
        for j in range(4):
            taps = pl.ds(((grp + j + 1) % 4) * 7, 7)
            total = parts[k, core, taps] + r1[k, taps].astype(f32)
            if j < 3:
                s2[k, j] = total.astype(bf16)
                second.append(
                    send(
                        s2.at[k, j], r2.at[k, j], ss2.at[k, j], rs2.at[k, j], across[j]
                    )
                )
            else:
                keep[k] = total

    def start_third(k):
        total = keep[k]
        for j in range(3):
            second[3 * k + j].wait_recv()
            total += r2[k, j].astype(f32)
        if k < 3:
            s3[k] = total.astype(bf16)
            third.append(send(s3.at[k], r3.at[k], ss3.at[k], rs3.at[k], along[k]))
        else:
            keep[k] = total

    start_first(0)
    start_first(1)
    start_second(0)
    start_first(2)
    bias_copies[0].wait_recv()
    sb[1] = sb[0] + rb[0]
    for k in range(3):
        bias_copies.append(
            send(sb.at[1], rb.at[1 + k], ssb.at[1 + k], rsb.at[1 + k], across[k])
        )
    start_second(1)
    start_first(3)
    start_second(2)
    start_third(0)
    start_second(3)
    start_third(1)
    for k in range(3):
        bias_copies[1 + k].wait_recv()
    sb[2] = (sb[1] + rb[1]) + (rb[2] + rb[3])
    for k in range(3):
        bias_copies.append(
            send(sb.at[2], rb.at[4 + k], ssb.at[4 + k], rsb.at[4 + k], along[k])
        )
    start_third(2)
    start_third(3)
    for k in range(3):
        bias_copies[4 + k].wait_recv()
    b_ref[...] = ((sb[2] + rb[4]) + (rb[5] + rb[6])) * scale
    total = keep[3]
    for k in range(3):
        third[k].wait_recv()
        total += r3[k].astype(f32)
    total = total * scale
    s4[...] = total
    fourth = [
        send(s4, r4.at[k], ss4.at[k], rs4.at[k], across[k]) for k in range(3)
    ]
    o_ref[grp] = total
    for k in range(3):
        fourth[k].wait_recv()
        o_ref[(grp + 3 - k) % 4] = r4[k]
    for copy in out + spread + swap + bias_copies + first + second + third + fourth:
        copy.wait_send()


def whole(counts, w, x, cot, bias, scale):
    bf16, f32 = jnp.bfloat16, jnp.float32
    sem = pltpu.SemaphoreType.DMA
    return pl.pallas_call(
        functools.partial(whole_kernel, scale),
        out_shape=(
            jax.ShapeDtypeStruct((4, 7, 16, 128), f32),
            jax.ShapeDtypeStruct((8, 128), f32),
        ),
        in_specs=[pl.BlockSpec(memory_space=pltpu.SMEM)]
        + [pl.BlockSpec(memory_space=pltpu.VMEM)]
        + [pl.BlockSpec(memory_space=pl.ANY)] * 2
        + [pl.BlockSpec(memory_space=pltpu.VMEM)],
        out_specs=[pl.BlockSpec(memory_space=pltpu.VMEM)] * 2,
        scratch_shapes=WORK
        + [
            pltpu.VMEM((8, 28, 16, 128), bf16),
            pltpu.VMEM((4, 2, 28, 16, 128), f32),
            pltpu.VMEM((4, 28, 16, 128), bf16),
            pltpu.VMEM((4, 28, 16, 128), bf16),
            pltpu.VMEM((4, 3, 7, 16, 128), bf16),
            pltpu.VMEM((4, 3, 7, 16, 128), bf16),
            pltpu.VMEM((4, 7, 16, 128), f32),
            pltpu.VMEM((3, 7, 16, 128), bf16),
            pltpu.VMEM((3, 7, 16, 128), bf16),
            pltpu.VMEM((7, 16, 128), f32),
            pltpu.VMEM((3, 7, 16, 128), f32),
            pltpu.VMEM((3, 8, 128), f32),
            pltpu.VMEM((7, 8, 128), f32),
            pltpu.VMEM((4, 576, 128), bf16),
            sem, pltpu.VMEM((576, 128), bf16), sem, sem((3, 3)), sem((3, 3)),
            sem((3,)), sem((3,)), sem((4,)), sem((4,)),
            sem((4,)), sem((4,)), sem((4, 3)), sem((4, 3)),
            sem((3,)), sem((3,)), sem((3,)), sem((3,)),
            sem((7,)), sem((7,)),
        ],
        compiler_params=pltpu.CompilerParams(
            collective_id=1, has_side_effects=True, vmem_limit_bytes=48 * 2**20
        ),
    )(counts, w, x, cot, bias)


def body(tiles, cotangent, weight, bias, counts):
    num_dev = lax.axis_size("dev")
    num_grp = lax.axis_size("grp")
    cap, frames, hl, wl, cin = tiles.shape
    cout = weight.shape[1]
    my_dev = lax.axis_index("dev")
    my_grp = lax.axis_index("grp")
    scale = 1.0 / math.sqrt(cap * num_dev * num_grp * frames * 4 * hl * wl)

    mine = weight.reshape(cin // num_dev, 27, cout).transpose(1, 0, 2)
    x = tiles.transpose(2, 3, 0, 1, 4).reshape(hl * wl * cap * frames, cin)
    cot = cotangent.reshape(cap, frames, hl, 2, wl, 2, cout).transpose(3, 5, 2, 4, 0, 1, 6)
    cot = cot.reshape(4, hl * wl * cap * frames, cout)

    share = cout // num_dev
    bias = bias.reshape(1, cout)
    if (num_grp, num_dev) == (4, 8):
        mine = jnp.pad(mine, ((0, 1), (0, 0), (0, 0)))
        done, total_b = whole(counts, mine, x, cot, bias, scale)
        done = done.reshape(28, 16, cout)
        part_w = done[:27].transpose(1, 0, 2).reshape(432, cout)
        part_b = lax.dynamic_slice_in_dim(total_b[0], my_dev * share, share, 0)
        return part_w, part_b
    gathered = lax.all_gather(mine, "dev", axis=0, tiled=False)
    if num_dev != 8:
        gathered = gathered.transpose(1, 0, 2, 3).reshape(27, 8, 16, cout)
        gathered = gathered.transpose(1, 0, 2, 3)
    count = lax.dynamic_slice_in_dim(counts, my_grp * num_dev + my_dev, 1)
    parts = terms(count, gathered, x, cot, bias)
    flat = parts[:, :27].transpose(0, 2, 1, 3).reshape(cin * 27, cout)
    part_w = lax.psum_scatter(flat, "dev", scatter_dimension=0, tiled=True)
    part_w = lax.psum(part_w, "grp")
    total_b = lax.psum(parts[0, 27, 0], ("grp", "dev"))
    part_b = lax.dynamic_slice_in_dim(total_b, my_dev * share, share, 0)
    return part_w * scale, part_b * scale


def solution(mesh):
    return jax.shard_map(
        body,
        mesh=mesh,
        in_specs=(
            P(("grp", "dev"), None, None, None, None),
            P(("grp", "dev"), None, None, None, None),
            P("dev", None),
            P(),
            P(),
        ),
        out_specs=(P("dev", None), P("dev")),
        check_vma=False,
    )
```
